32 devices in a mesh: row: 4 (over z), col: 2 (over x), depth: 4 (over y, core).
Axes of the slice: x: 2, y: 2, z: 4, core: 2. Of those that a mesh axis runs over, the one named last changes fastest.
Arguments:
- amplitudes: bfloat16 [3200, 7200], P('row', ('col', 'depth')), may hold values from -6 to 6
- integrals: bfloat16 [7200, 4096], P('row', ('col', 'depth')), may hold values from -0.0625 to 0.0625
- cycle_integrals: bfloat16 [256, 256], P('row'), as said below
- occ_irrep: int32 [100], replicated, may hold values from 0 to 7
- vir_irrep: int32 [900], replicated, may hold values from 0 to 7
Outputs:
- ladder: bfloat16 [3200, 4096], P('row', ('col', 'depth'))
- cycle: bfloat16 [256, 57600], P('row', ('col', 'depth'))
The draws below stay inside these ranges and needn't reach their ends.
Inputs may be any that keep to these rules, and one draw needn't show every extreme that they name: cycle_integrals equals its transpose.
All inputs are finite; a program needn't handle non-finite values.
Results may differ from the reference program's by a relative error of at most 0.001.
Values may be sent and summed in bfloat16 or wider, within the bound.
A program may use at most 128 MiB of HBM per device.

```python
import math
import jax
import jax.numpy as jnp

NO = 100
NV = 900
BW = 512
JW = 64
CW = 8
IW = 32
AW = 8
K = 7200


def draw_cycle_integrals(key, part):
    entries = IW * CW
    sample = jax.random.normal(key, (entries, entries), jnp.float32)
    return ((sample + sample.T) * (0.70710678 / math.sqrt(entries))).astype(jnp.bfloat16)


def set_ends(values, own_key, smallest, top_value):
    place = [jax.random.randint(jax.random.fold_in(own_key, axis), (), 0, length) for axis, length in enumerate(values.shape)]
    longest = values.shape.index(max(values.shape))
    beside = place[:longest] + [(place[longest] + 1) % values.shape[longest]] + place[longest + 1:]
    return values.at[tuple(place)].set(smallest).at[tuple(beside)].set(top_value)


def block_levels(stream_key, shape, cuts, least, top_value):
    gain, own = 1.0, jax.random.fold_in(stream_key, 6)
    for axis_at, shards_of in cuts:
        steps = jnp.exp(jax.random.uniform(jax.random.fold_in(own, axis_at), (shards_of,), jnp.float32, least / len(cuts), top_value / len(cuts)))
        gain = gain * jnp.repeat(steps, shape[axis_at] // shards_of).reshape([-1 if axis == axis_at else 1 for axis in range(len(shape))])
    return gain


def normal_values(rng, dims, scale, most, split=(), dtype=jnp.bfloat16):
    factor_of = block_levels(rng, dims, split, -0.22, 0.18) if split else 1.0
    result = jax.random.normal(rng, dims, jnp.float32) * scale * factor_of
    return jnp.minimum(jnp.maximum(result, -most), most).astype(dtype)


def setup_inputs(seed: int = 0) -> dict:
    keys = jax.random.split(jax.random.key(seed), 6)
    return {
        "amplitudes": normal_values(keys[0], (IW * NO, K), 1.0, 6.0, ((0, 4), (1, 8))),
        "integrals": normal_values(keys[1], (K, AW * BW), K ** -0.5, 0.0625, ((0, 4), (1, 8))),
        "cycle_integrals": draw_cycle_integrals(jax.random.fold_in(keys[5], 71), 0),
        "occ_irrep": set_ends(jax.random.randint(keys[3], (NO,), 0, 8), jax.random.fold_in(keys[3], 1), 0, 7).astype(jnp.int32),
        "vir_irrep": set_ends(jax.random.randint(keys[4], (NV,), 0, 8), jax.random.fold_in(keys[4], 1), 0, 7).astype(jnp.int32),
    }


def label_bits(labels):
    return jnp.stack([labels % 2, (labels // 2) % 2, (labels // 4) % 2])


def reference(amplitudes, integrals, cycle_integrals, occ_irrep, vir_irrep):
    ladder = jnp.dot(amplitudes, integrals, preferred_element_type=jnp.float32).astype(jnp.bfloat16)
    regrouped = amplitudes.reshape(IW, NO, CW, NV)[:, :JW].transpose(0, 2, 1, 3).reshape(IW * CW, JW * NV)
    cycle_sum = jnp.dot(cycle_integrals, regrouped, preferred_element_type=jnp.float32)
    occ_bits = label_bits(occ_irrep)
    vir_bits = label_bits(vir_irrep)
    odd_count = jnp.zeros((IW * CW, JW * NV), jnp.int32)
    for digit in range(3):
        row_bits = (occ_bits[digit, :IW, None] + vir_bits[digit, None, :CW]).reshape(IW * CW)
        column_bits = (occ_bits[digit, :JW, None] + vir_bits[digit, None, :]).reshape(JW * NV)
        odd_count = odd_count + (row_bits[:, None] + column_bits[None, :]) % 2
    cycle = jnp.where(odd_count == 0, cycle_sum, jnp.float32(0.0)).astype(jnp.bfloat16)
    return ladder, cycle
```

```python
import functools

import jax
import jax.numpy as jnp
from jax import lax
from jax.experimental import pallas as pl
from jax.experimental.pallas import tpu as pltpu
from jax.sharding import PartitionSpec as P

NO = 100
NV = 900
JW = 64
CW = 8
MESH = pl.DeviceIdType.MESH


def masks(rows_here, columns, occ_irrep, vir_irrep):
    occ_rows = rows_here // CW
    occ_cols = columns // NV
    occ_i = lax.dynamic_slice(occ_irrep, (lax.axis_index("row") * occ_rows,), (occ_rows,))
    occ_j = lax.dynamic_slice(occ_irrep, (lax.axis_index(("col", "depth")) * occ_cols,), (occ_cols,))
    row_label = (occ_i[:, None] ^ vir_irrep[None, :CW]).reshape(rows_here, 1)
    col_label = (occ_j[:, None] ^ vir_irrep[None, :]).reshape(1, columns)
    return row_label, col_label


def general(amplitudes, integrals, cycle_integrals, occ_irrep, vir_irrep):
    rows_here = amplitudes.shape[0]
    occ_block = rows_here // NO
    local_cols = amplitudes.shape[1]
    regroup_in = amplitudes.reshape(occ_block, NO, local_cols)[:, :JW, :]
    spread = lax.all_to_all(regroup_in, ("col", "depth"), split_axis=1, concat_axis=2, tiled=True)
    occ_here = spread.shape[1]
    columns = occ_here * NV
    ordered = (
        spread.reshape(occ_block, occ_here, CW, NV)
        .transpose(0, 2, 1, 3)
        .reshape(occ_block * CW, columns)
    )
    everyone = lax.all_gather(ordered, "row", axis=0, tiled=True)
    integ_all = lax.all_gather(integrals, "row", axis=0, tiled=True)
    ladder = jnp.dot(
        lax.all_gather(amplitudes, ("col", "depth"), axis=1, tiled=True),
        integ_all,
        preferred_element_type=jnp.float32,
    ).astype(jnp.bfloat16)
    cycle_sum = jnp.dot(cycle_integrals, everyone, preferred_element_type=jnp.float32)
    row_label, col_label = masks(cycle_integrals.shape[0], columns, occ_irrep, vir_irrep)
    cycle = jnp.where(row_label == col_label, cycle_sum, jnp.float32(0.0)).astype(jnp.bfloat16)
    return ladder, cycle


def kernel(nz, a_ref, b_ref, s_ref, ci_ref, rl_ref, cl_ref, lad_ref, cyc_ref,
           aall, ball, rall, acc, loc_sem, s_send, s_recv, a_send, a_recv, z_send, z_recv):
    z = lax.axis_index("row")
    x = lax.axis_index("col")
    dep = lax.axis_index("depth")
    y, core = dep // 2, lax.rem(dep, 2)
    nd = 4
    npl = 8
    p = x * nd + dep
    partner = {"depth": y * 2 + 1 - core}
    xn = {"col": 1 - x}
    yn = {"depth": (1 - y) * 2 + core}

    def remote(src, dst, ss, rs, dev):
        return pltpu.make_async_remote_copy(
            src_ref=src, dst_ref=dst, send_sem=ss, recv_sem=rs, device_id=dev, device_id_type=MESH
        )

    def peer(i):
        q = lax.rem(p + i, npl)
        return q, {"col": q // nd, "depth": lax.rem(q, nd)}

    barrier = pltpu.get_barrier_semaphore()
    for i in range(1, npl):
        pl.semaphore_signal(barrier, inc=1, device_id=peer(i)[1], device_id_type=MESH)

    @pl.when(z > 0)
    def _():
        pl.semaphore_signal(barrier, inc=1, device_id={"row": z - 1}, device_id_type=MESH)

    @pl.when(z < nz - 1)
    def _():
        pl.semaphore_signal(barrier, inc=1, device_id={"row": z + 1}, device_id_type=MESH)

    own_a = pltpu.make_async_copy(a_ref, aall.at[p], loc_sem.at[0])
    own_b = pltpu.make_async_copy(b_ref, ball.at[z], loc_sem.at[1])
    own_s = pltpu.make_async_copy(s_ref.at[p], rall.at[z, p], loc_sem.at[2])
    own_a.start()
    own_b.start()
    own_s.start()

    greeted = npl + 1 - (z == 0).astype(jnp.int32) - (z == nz - 1).astype(jnp.int32)
    pl.semaphore_wait(barrier, greeted)

    def z_dst(item, s):
        return rall.at[s] if item == 2 else ball.at[s, item]

    def z_copy(item, s, up, src=None):
        dst = z_dst(item, s)
        d = 1 if up else 0
        dev = {"row": z + 1} if up else {"row": z - 1}
        return remote(dst if src is None else src, dst, z_send.at[item, s, d], z_recv.at[item, s], dev)

    def z_out(item, s, up, start, src=None):
        edge = (z < nz - 1) if up else (z > 0)

        @pl.when(edge)
        def _():
            c = z_copy(item, s, up, src)
            if start:
                c.start()
            else:
                c.wait_send()

    def z_both(item, start, src=None):
        z_out(item, z, True, start, src)
        z_out(item, z, False, start, src)

    for i in range(1, npl):
        q, dev = peer(i)
        remote(s_ref.at[q], rall.at[z, p], s_send.at[i], s_recv.at[p], dev).start()
    z_both(0, True, b_ref.at[0])
    z_both(1, True, b_ref.at[1])

    def a_copy(q, h, way, src=None):
        dst = aall.at[q, h]
        k = {"p": 0, "x": 1, "y": 2}[way]
        dev = {"p": partner, "x": xn, "y": yn}[way]
        return remote(dst if src is None else src, dst, a_send.at[k, q, h], a_recv.at[q, h], dev)

    q_x = (1 - x) * nd + dep
    q_y = x * nd + (1 - y) * 2 + core
    q_d = (1 - x) * nd + (1 - y) * 2 + core
    sends = []

    def a_start(q, h, way, src=None):
        c = a_copy(q, h, way, src)
        c.start()
        sends.append(c)

    for h in range(2):
        for way in ("x", "y", "p"):
            a_start(p, h, way, a_ref.at[h])

    own_s.wait()
    for i in range(1, npl):
        q, dev = peer(i)
        remote(s_ref.at[p], rall.at[z, q], s_send.at[i], s_recv.at[q], dev).wait_recv()
    z_both(2, True)

    a_copy(q_x, 0, "x").wait_recv()
    a_start(q_x, 0, "y")
    a_start(q_x, 0, "p")
    a_copy(q_y, 0, "y").wait_recv()
    a_start(q_y, 0, "p")
    a_copy(q_y, 1, "y").wait_recv()
    a_start(q_y, 1, "x")
    a_start(q_y, 1, "p")
    a_copy(q_x, 1, "x").wait_recv()
    a_start(q_x, 1, "p")

    def arrive(item, dist):
        @pl.when(z - dist >= 0)
        def _():
            z_copy(item, z - dist, True).wait_recv()
            z_out(item, z - dist, True, True)

        @pl.when(z + dist < nz)
        def _():
            z_copy(item, z + dist, False).wait_recv()
            z_out(item, z + dist, False, True)

    arrive(0, 1)
    a_copy(q_d, 0, "y").wait_recv()
    a_start(q_d, 0, "p")
    a_copy(q_d, 1, "x").wait_recv()
    a_start(q_d, 1, "p")
    arrive(1, 1)
    for q in (p, q_x, q_y, q_d):
        other = q + 1 - 2 * core
        for h in range(2):
            a_copy(other, h, "p").wait_recv()
    own_a.wait()
    own_b.wait()
    per = npl // nz
    acc[...] = jnp.zeros_like(acc)

    def ladder_part(s, item):
        def body(n, carry):
            kb, h = n // 2, lax.rem(n, 2)
            acc[h, item] += jnp.dot(
                aall[s * per + kb, h], ball[s, item, kb], preferred_element_type=jnp.float32
            )
            return carry

        lax.fori_loop(0, 2 * per, body, 0)

    cols = cyc_ref.shape[1]
    width = 1024
    bounds = [(c, min(c + width, cols)) for c in range(0, cols, width)]

    ladder_part(z, 0)
    ladder_part(z, 1)

    def consume(item, dist):
        @pl.when(z - dist >= 0)
        def _():
            ladder_part(z - dist, item)

        @pl.when(z + dist < nz)
        def _():
            ladder_part(z + dist, item)

    for dist in range(1, nz):
        if dist > 1:
            arrive(0, dist)
            consume(0, dist)
            arrive(1, dist)
            consume(1, dist)
        else:
            consume(0, dist)
            consume(1, dist)
        arrive(2, dist)

    hr = lad_ref.shape[0] // 2
    hc = lad_ref.shape[1] // 2
    for h in range(2):
        for item in range(2):
            lad_ref[h * hr:(h + 1) * hr, item * hc:(item + 1) * hc] = acc[h, item].astype(lad_ref.dtype)
    rows = rall.shape[0] * rall.shape[1] * rall.shape[2]
    for lo, hi in bounds:
        r = rall[:, :, :, lo:hi].reshape(rows, hi - lo)
        total = jnp.dot(ci_ref[...], r, preferred_element_type=jnp.float32)
        keep = rl_ref[...] == cl_ref[:, lo:hi]
        cyc_ref[:, lo:hi] = jnp.where(keep, total, 0.0).astype(cyc_ref.dtype)

    for i in range(1, npl):
        q, dev = peer(i)
        remote(s_ref.at[q], rall.at[z, p], s_send.at[i], s_recv.at[p], dev).wait_send()
    for c in sends:
        c.wait_send()
    z_both(0, False, b_ref.at[0])
    z_both(1, False, b_ref.at[1])
    z_both(2, False)
    for dist in range(1, nz):
        for item in range(3):
            @pl.when(z - dist >= 0)
            def _():
                z_out(item, z - dist, True, False)

            @pl.when(z + dist < nz)
            def _():
                z_out(item, z + dist, False, False)


def shards(nz, npl, amplitudes, integrals, cycle_integrals, occ_irrep, vir_irrep):
    rows, kb = amplitudes.shape
    occ = rows // NO
    n = integrals.shape[1]
    per = npl // nz
    occ_here = JW // npl
    columns = occ_here * NV
    crow = cycle_integrals.shape[0]
    a = amplitudes.reshape(2, rows // 2, kb)
    b = integrals.reshape(per, kb, 2, n // 2).transpose(2, 0, 1, 3)
    s = (
        amplitudes.reshape(occ, NO, kb)[:, :JW]
        .reshape(occ, npl, occ_here, kb)
        .transpose(1, 0, 2, 3)
        .reshape(npl, occ, columns)
    )
    ci = cycle_integrals.reshape(crow, nz, occ, CW).transpose(0, 1, 3, 2).reshape(crow, -1)
    row_label, col_label = masks(crow, columns, occ_irrep, vir_irrep)
    bf = jnp.bfloat16
    dma = pltpu.SemaphoreType.DMA
    return pl.pallas_call(
        functools.partial(kernel, nz),
        out_shape=(
            jax.ShapeDtypeStruct((rows, n), bf),
            jax.ShapeDtypeStruct((crow, columns), bf),
        ),
        in_specs=[pl.BlockSpec(memory_space=pltpu.VMEM)] * 6,
        out_specs=(pl.BlockSpec(memory_space=pltpu.VMEM),) * 2,
        scratch_shapes=[
            pltpu.VMEM((npl, 2, rows // 2, kb), bf),
            pltpu.VMEM((nz, 2, per, kb, n // 2), bf),
            pltpu.VMEM((nz, npl, occ, columns), bf),
            pltpu.VMEM((2, 2, rows // 2, n // 2), jnp.float32),
            dma((3,)),
            dma((npl,)),
            dma((npl,)),
            dma((3, npl, 2)),
            dma((npl, 2)),
            dma((3, nz, 2)),
            dma((3, nz)),
        ],
        compiler_params=pltpu.CompilerParams(
            collective_id=0, has_side_effects=True, vmem_limit_bytes=60 * 1024 * 1024
        ),
    )(a, b, s, ci, row_label, col_label)


def solution(mesh):
    nz, nx, nd = mesh.shape["row"], mesh.shape["col"], mesh.shape["depth"]
    npl = nx * nd
    if nx == 2 and nd == 4 and npl == CW and npl % nz == 0:
        body = functools.partial(shards, nz, npl)
    else:
        body = general
    in_specs = (P("row", ("col", "depth")), P("row", ("col", "depth")), P("row", None), P(), P())
    out_specs = (P("row", ("col", "depth")), P("row", ("col", "depth")))
    return jax.shard_map(body, mesh=mesh, in_specs=in_specs, out_specs=out_specs, check_vma=False)
```

```python
import functools

import jax
import jax.numpy as jnp
from jax import lax
from jax.experimental import pallas as pl
from jax.experimental.pallas import tpu as pltpu
from jax.sharding import PartitionSpec as P

NO = 100
NV = 900
JW = 64
CW = 8
MESH = pl.DeviceIdType.MESH


def masks(rows_here, columns, occ_irrep, vir_irrep):
    occ_rows = rows_here // CW
    occ_cols = columns // NV
    occ_i = lax.dynamic_slice(occ_irrep, (lax.axis_index("row") * occ_rows,), (occ_rows,))
    occ_j = lax.dynamic_slice(occ_irrep, (lax.axis_index(("col", "depth")) * occ_cols,), (occ_cols,))
    row_label = (occ_i[:, None] ^ vir_irrep[None, :CW]).reshape(rows_here, 1)
    col_label = (occ_j[:, None] ^ vir_irrep[None, :]).reshape(1, columns)
    return row_label, col_label


def general(amplitudes, integrals, cycle_integrals, occ_irrep, vir_irrep):
    rows_here = amplitudes.shape[0]
    occ_block = rows_here // NO
    local_cols = amplitudes.shape[1]
    regroup_in = amplitudes.reshape(occ_block, NO, local_cols)[:, :JW, :]
    spread = lax.all_to_all(regroup_in, ("col", "depth"), split_axis=1, concat_axis=2, tiled=True)
    occ_here = spread.shape[1]
    columns = occ_here * NV
    ordered = (
        spread.reshape(occ_block, occ_here, CW, NV)
        .transpose(0, 2, 1, 3)
        .reshape(occ_block * CW, columns)
    )
    everyone = lax.all_gather(ordered, "row", axis=0, tiled=True)
    integ_all = lax.all_gather(integrals, "row", axis=0, tiled=True)
    ladder = jnp.dot(
        lax.all_gather(amplitudes, ("col", "depth"), axis=1, tiled=True),
        integ_all,
        preferred_element_type=jnp.float32,
    ).astype(jnp.bfloat16)
    cycle_sum = jnp.dot(cycle_integrals, everyone, preferred_element_type=jnp.float32)
    row_label, col_label = masks(cycle_integrals.shape[0], columns, occ_irrep, vir_irrep)
    cycle = jnp.where(row_label == col_label, cycle_sum, jnp.float32(0.0)).astype(jnp.bfloat16)
    return ladder, cycle


def kernel(a_ref, b_ref, s_ref, ci_ref, rl_ref, cl_ref, lad_ref, cyc_ref,
           aall, oall, ball, rall, acc, pacc, pin, loc_sem, s_send, s_recv,
           a_send, a_recv, o_send, o_recv, z_send, z_recv, n_send, p_send, p_recv):
    z = lax.axis_index("row")
    x = lax.axis_index("col")
    dep = lax.axis_index("depth")
    y, core = dep // 2, lax.rem(dep, 2)
    nd = 4
    npl = 8
    nz = rall.shape[0]
    per = npl // nz
    p = x * nd + dep
    partner = {"depth": y * 2 + 1 - core}
    xn = {"col": 1 - x}
    yn = {"depth": (1 - y) * 2 + core}
    inward = jnp.where(z < nz // 2, 1, -1)
    outer = (z == 0) | (z == nz - 1)
    inner = jnp.logical_not(outer)
    to_in = {"row": z + inward}
    to_out = {"row": z - inward}

    def remote(src, dst, ss, rs, dev):
        return pltpu.make_async_remote_copy(
            src_ref=src, dst_ref=dst, send_sem=ss, recv_sem=rs, device_id=dev, device_id_type=MESH
        )

    def peer(i):
        q = lax.rem(p + i, npl)
        return q, {"col": q // nd, "depth": lax.rem(q, nd)}

    barrier = pltpu.get_barrier_semaphore()
    for i in range(1, npl):
        pl.semaphore_signal(barrier, inc=1, device_id=peer(i)[1], device_id_type=MESH)
    pl.semaphore_signal(barrier, inc=1, device_id=to_in, device_id_type=MESH)

    @pl.when(inner)
    def _():
        pl.semaphore_signal(barrier, inc=1, device_id=to_out, device_id_type=MESH)

    own_a = pltpu.make_async_copy(a_ref, aall.at[p], loc_sem.at[0])
    own_b = pltpu.make_async_copy(b_ref, ball.at[z], loc_sem.at[1])
    own_s = pltpu.make_async_copy(s_ref.at[p], rall.at[z, p], loc_sem.at[2])
    own_a.start()
    own_b.start()
    own_s.start()
    pl.semaphore_wait(barrier, npl + inner.astype(jnp.int32))

    common, middle, ends = [], [], []

    def begin(kept, make, *args, **kw):
        make(*args, **kw).start()
        kept.append(functools.partial(make, *args, **kw))

    def z_copy(item, k, outwards=False, src=None):
        s = z + k * inward
        dst = rall.at[s] if item == 2 else ball.at[s, item]
        d = 1 if outwards else 0
        return remote(dst if src is None else src(), dst, z_send.at[item, s, d],
                      z_recv.at[item, s], to_out if outwards else to_in)

    def arrived(item, k):
        z_copy(item, k).wait_recv()

    def o_in(h):
        return remote(a_ref.at[h], oall.at[p, h], n_send.at[h], o_recv.at[p, h], to_in)

    def s_out(i):
        q, dev = peer(i)
        return remote(s_ref.at[q], rall.at[z, p], s_send.at[i], s_recv.at[p], dev)

    for i in range(1, npl):
        begin(common, s_out, i)

    @pl.when(outer)
    def _():
        for h in range(2):
            begin(ends, o_in, h)

    begin(common, z_copy, 1, 0, src=lambda: b_ref.at[1])

    @pl.when(inner)
    def _():
        begin(middle, z_copy, 1, 0, True, src=lambda: b_ref.at[1])

    q_x = (1 - x) * nd + dep
    q_y = x * nd + (1 - y) * 2 + core
    q_d = (1 - x) * nd + (1 - y) * 2 + core

    def plane(buf, send, recv, kept):
        def copy(q, h, way, src=None):
            n = {"p": 0, "x": 1, "y": 2}[way]
            dev = {"p": partner, "x": xn, "y": yn}[way]
            dst = buf.at[q, h]
            return remote(dst if src is None else src(), dst, send.at[n, q, h], recv.at[q, h], dev)

        def first(src):
            for h in range(2):
                for way in ("x", "y", "p"):
                    begin(kept, copy, p, h, way, functools.partial(src, h))

        def second():
            copy(q_x, 0, "x").wait_recv()
            begin(kept, copy, q_x, 0, "y")
            begin(kept, copy, q_x, 0, "p")
            copy(q_y, 0, "y").wait_recv()
            begin(kept, copy, q_y, 0, "p")
            copy(q_y, 1, "y").wait_recv()
            begin(kept, copy, q_y, 1, "x")
            begin(kept, copy, q_y, 1, "p")
            copy(q_x, 1, "x").wait_recv()
            begin(kept, copy, q_x, 1, "p")

        def third():
            copy(q_d, 0, "y").wait_recv()
            begin(kept, copy, q_d, 0, "p")
            copy(q_d, 1, "x").wait_recv()
            begin(kept, copy, q_d, 1, "p")

        def last():
            for q in (p, q_x, q_y, q_d):
                other = q + 1 - 2 * core
                for h in range(2):
                    copy(other, h, "p").wait_recv()

        return first, second, third, last

    a_first, a_second, a_third, a_last = plane(aall, a_send, a_recv, common)
    o_first, o_second, o_third, o_last = plane(oall, o_send, o_recv, middle)

    a_first(lambda h: a_ref.at[h])

    own_s.wait()
    for i in range(1, npl):
        q, dev = peer(i)
        remote(s_ref.at[p], rall.at[z, q], s_send.at[i], s_recv.at[q], dev).wait_recv()
    begin(common, z_copy, 2, 0)

    @pl.when(inner)
    def _():
        begin(middle, z_copy, 2, 0, True)

    begin(common, z_copy, 0, 0, src=lambda: b_ref.at[0])

    a_second()
    acc[...] = jnp.zeros_like(acc)
    pacc[...] = jnp.zeros_like(pacc)

    def ladder_part(k, item):
        s = z + k * inward

        def body(n, carry):
            kb, h = n // 2, lax.rem(n, 2)
            acc[h, item] += jnp.dot(
                aall[s * per + kb, h], ball[s, item, kb], preferred_element_type=jnp.float32
            )
            return carry

        lax.fori_loop(0, 2 * per, body, 0)

    def other_part(k, h):
        s = z + k * inward

        def body(kb, carry):
            pacc[h] += jnp.dot(
                oall[s * per + kb, h], ball[s, 0, kb], preferred_element_type=jnp.float32
            )
            return carry

        lax.fori_loop(0, per, body, 0)

    def p_copy(h):
        return remote(pacc.at[h], pin.at[h], p_send.at[h], p_recv.at[h], to_out)

    @pl.when(inner)
    def _():
        for h in range(2):
            o_in(h).wait_recv()
        o_first(lambda h: oall.at[p, h])
        arrived(1, 1)
        begin(middle, z_copy, 1, 1, True)
        arrived(2, 1)
        begin(middle, z_copy, 2, 1, True)

    a_third()

    @pl.when(inner)
    def _():
        arrived(1, -1)
        begin(middle, z_copy, 1, -1)

    a_last()
    own_a.wait()
    own_b.wait()
    ladder_part(0, 0)
    ladder_part(0, 1)

    @pl.when(inner)
    def _():
        arrived(2, -1)
        begin(middle, z_copy, 2, -1)
        arrived(1, 2)
        begin(middle, z_copy, 1, 2, True)
        o_second()
        arrived(0, -1)
        begin(middle, z_copy, 0, -1)
        arrived(2, 2)
        begin(middle, z_copy, 2, 2, True)
        o_third()
        ladder_part(-1, 0)
        ladder_part(-1, 1)
        ladder_part(1, 1)
        ladder_part(2, 1)
        arrived(0, 1)
        ladder_part(1, 0)
        o_last()
        for k in (0, 1):
            for h in range(2):
                other_part(k, h)

    @pl.when(outer)
    def _():
        for k in range(1, nz):
            arrived(1, k)
            ladder_part(k, 1)
            arrived(2, k)

    cols = cyc_ref.shape[1]
    width = 1024
    bounds = [(c, min(c + width, cols)) for c in range(0, cols, width)]
    rows = rall.shape[0] * rall.shape[1] * rall.shape[2]
    for lo, hi in bounds:
        r = rall[:, :, :, lo:hi].reshape(rows, hi - lo)
        total = jnp.dot(ci_ref[...], r, preferred_element_type=jnp.float32)
        keep = rl_ref[...] == cl_ref[:, lo:hi]
        cyc_ref[:, lo:hi] = jnp.where(keep, total, 0.0).astype(cyc_ref.dtype)

    @pl.when(inner)
    def _():
        arrived(0, 2)
        for h in range(2):
            other_part(2, h)
            begin(middle, p_copy, h)
        ladder_part(2, 0)

    hr = lad_ref.shape[0] // 2
    hc = lad_ref.shape[1] // 2
    for h in range(2):
        lad_ref[h * hr:(h + 1) * hr, hc:] = acc[h, 1].astype(lad_ref.dtype)

    @pl.when(inner)
    def _():
        for h in range(2):
            lad_ref[h * hr:(h + 1) * hr, :hc] = acc[h, 0].astype(lad_ref.dtype)

    @pl.when(outer)
    def _():
        for h in range(2):
            p_copy(h).wait_recv()
            lad_ref[h * hr:(h + 1) * hr, :hc] = (acc[h, 0] + pin[h]).astype(lad_ref.dtype)

    for c in common:
        c().wait_send()

    @pl.when(inner)
    def _():
        for c in middle:
            c().wait_send()

    @pl.when(outer)
    def _():
        for c in ends:
            c().wait_send()


def shards(nz, npl, amplitudes, integrals, cycle_integrals, occ_irrep, vir_irrep):
    rows, kb = amplitudes.shape
    occ = rows // NO
    n = integrals.shape[1]
    per = npl // nz
    occ_here = JW // npl
    columns = occ_here * NV
    crow = cycle_integrals.shape[0]
    a = amplitudes.reshape(2, rows // 2, kb)
    b = integrals.reshape(per, kb, 2, n // 2).transpose(2, 0, 1, 3)
    s = (
        amplitudes.reshape(occ, NO, kb)[:, :JW]
        .reshape(occ, npl, occ_here, kb)
        .transpose(1, 0, 2, 3)
        .reshape(npl, occ, columns)
    )
    ci = cycle_integrals.reshape(crow, nz, occ, CW).transpose(0, 1, 3, 2).reshape(crow, -1)
    row_label, col_label = masks(crow, columns, occ_irrep, vir_irrep)
    bf = jnp.bfloat16
    dma = pltpu.SemaphoreType.DMA
    return pl.pallas_call(
        kernel,
        out_shape=(
            jax.ShapeDtypeStruct((rows, n), bf),
            jax.ShapeDtypeStruct((crow, columns), bf),
        ),
        in_specs=[pl.BlockSpec(memory_space=pltpu.VMEM)] * 6,
        out_specs=(pl.BlockSpec(memory_space=pltpu.VMEM),) * 2,
        scratch_shapes=[
            pltpu.VMEM((npl, 2, rows // 2, kb), bf),
            pltpu.VMEM((npl, 2, rows // 2, kb), bf),
            pltpu.VMEM((nz, 2, per, kb, n // 2), bf),
            pltpu.VMEM((nz, npl, occ, columns), bf),
            pltpu.VMEM((2, 2, rows // 2, n // 2), jnp.float32),
            pltpu.VMEM((2, rows // 2, n // 2), jnp.float32),
            pltpu.VMEM((2, rows // 2, n // 2), jnp.float32),
            dma((3,)),
            dma((npl,)),
            dma((npl,)),
            dma((3, npl, 2)),
            dma((npl, 2)),
            dma((3, npl, 2)),
            dma((npl, 2)),
            dma((3, nz, 2)),
            dma((3, nz)),
            dma((2,)),
            dma((2,)),
            dma((2,)),
        ],
        compiler_params=pltpu.CompilerParams(
            collective_id=0, has_side_effects=True, vmem_limit_bytes=62 * 1024 * 1024
        ),
    )(a, b, s, ci, row_label, col_label)


def solution(mesh):
    nz, nx, nd = mesh.shape["row"], mesh.shape["col"], mesh.shape["depth"]
    npl = nx * nd
    if nx == 2 and nd == 4 and npl == CW and nz == 4:
        body = functools.partial(shards, nz, npl)
    else:
        body = general
    in_specs = (P("row", ("col", "depth")), P("row", ("col", "depth")), P("row", None), P(), P())
    out_specs = (P("row", ("col", "depth")), P("row", ("col", "depth")))
    return jax.shard_map(body, mesh=mesh, in_specs=in_specs, out_specs=out_specs, check_vma=False)
```

```python
import functools

import jax
import jax.numpy as jnp
from jax import lax
from jax.experimental import pallas as pl
from jax.experimental.pallas import tpu as pltpu
from jax.sharding import PartitionSpec as P

NO = 100
NV = 900
JW = 64
CW = 8
MESH = pl.DeviceIdType.MESH


def masks(rows_here, columns, occ_irrep, vir_irrep):
    occ_rows = rows_here // CW
    occ_cols = columns // NV
    occ_i = lax.dynamic_slice(occ_irrep, (lax.axis_index("row") * occ_rows,), (occ_rows,))
    occ_j = lax.dynamic_slice(occ_irrep, (lax.axis_index(("col", "depth")) * occ_cols,), (occ_cols,))
    row_label = (occ_i[:, None] ^ vir_irrep[None, :CW]).reshape(rows_here, 1)
    col_label = (occ_j[:, None] ^ vir_irrep[None, :]).reshape(1, columns)
    return row_label, col_label


def general(amplitudes, integrals, cycle_integrals, occ_irrep, vir_irrep):
    rows_here = amplitudes.shape[0]
    occ_block = rows_here // NO
    local_cols = amplitudes.shape[1]
    regroup_in = amplitudes.reshape(occ_block, NO, local_cols)[:, :JW, :]
    spread = lax.all_to_all(regroup_in, ("col", "depth"), split_axis=1, concat_axis=2, tiled=True)
    occ_here = spread.shape[1]
    columns = occ_here * NV
    ordered = (
        spread.reshape(occ_block, occ_here, CW, NV)
        .transpose(0, 2, 1, 3)
        .reshape(occ_block * CW, columns)
    )
    everyone = lax.all_gather(ordered, "row", axis=0, tiled=True)
    integ_all = lax.all_gather(integrals, "row", axis=0, tiled=True)
    ladder = jnp.dot(
        lax.all_gather(amplitudes, ("col", "depth"), axis=1, tiled=True),
        integ_all,
        preferred_element_type=jnp.float32,
    ).astype(jnp.bfloat16)
    cycle_sum = jnp.dot(cycle_integrals, everyone, preferred_element_type=jnp.float32)
    row_label, col_label = masks(cycle_integrals.shape[0], columns, occ_irrep, vir_irrep)
    cycle = jnp.where(row_label == col_label, cycle_sum, jnp.float32(0.0)).astype(jnp.bfloat16)
    return ladder, cycle


def kernel(a_ref, b_ref, s_ref, ci_ref, rl_ref, cl_ref, lad_ref, cyc_ref,
           aall, oall, ball, rall, acc, pacc, pin, loc_sem, s_send, s_recv,
           a_send, a_recv, o_send, o_recv, z_send, z_recv, n_send, p_send, p_recv):
    z = lax.axis_index("row")
    x = lax.axis_index("col")
    dep = lax.axis_index("depth")
    y, core = dep // 2, lax.rem(dep, 2)
    nd = 4
    npl = 8
    nz = rall.shape[0]
    per = npl // nz
    p = x * nd + dep
    partner = {"depth": y * 2 + 1 - core}
    xn = {"col": 1 - x}
    yn = {"depth": (1 - y) * 2 + core}
    inward = jnp.where(z < nz // 2, 1, -1)
    outer = (z == 0) | (z == nz - 1)
    inner = jnp.logical_not(outer)
    to_in = {"row": z + inward}
    to_out = {"row": z - inward}

    def remote(src, dst, ss, rs, dev):
        return pltpu.make_async_remote_copy(
            src_ref=src, dst_ref=dst, send_sem=ss, recv_sem=rs, device_id=dev, device_id_type=MESH
        )

    def peer(i):
        q = lax.rem(p + i, npl)
        return q, {"col": q // nd, "depth": lax.rem(q, nd)}

    barrier = pltpu.get_barrier_semaphore()
    for i in range(1, npl):
        pl.semaphore_signal(barrier, inc=1, device_id=peer(i)[1], device_id_type=MESH)
    pl.semaphore_signal(barrier, inc=1, device_id=to_in, device_id_type=MESH)

    @pl.when(inner)
    def _():
        pl.semaphore_signal(barrier, inc=1, device_id=to_out, device_id_type=MESH)

    own_a = pltpu.make_async_copy(a_ref, aall.at[p], loc_sem.at[0])
    wide = ball.shape[3]
    nc = ball.shape[1]
    direct = nc - 1

    def b_part(c):
        return b_ref.at[:, c * wide:(c + 1) * wide]

    own_b = [pltpu.make_async_copy(b_part(c), ball.at[z, c], loc_sem.at[2 + c]) for c in range(nc)]
    own_s = pltpu.make_async_copy(s_ref.at[p], rall.at[z, p], loc_sem.at[1])
    own_a.start()
    for c in own_b:
        c.start()
    own_s.start()
    pl.semaphore_wait(barrier, npl + inner.astype(jnp.int32))

    half = npl // 2
    common, middle, ends = [], [], []

    def begin(kept, make, *args, **kw):
        make(*args, **kw).start()
        kept.append(functools.partial(make, *args, **kw))

    def z_copy(item, k, outwards=False, src=None):
        s = z + k * inward
        if item < nc:
            dst = ball.at[s, item]
        else:
            dst = rall.at[s, pl.ds((item - nc) * half, half)]
        d = 1 if outwards else 0
        return remote(dst if src is None else src(), dst, z_send.at[item, s, d],
                      z_recv.at[item, s], to_out if outwards else to_in)

    def arrived(item, k):
        z_copy(item, k).wait_recv()

    def o_in(h):
        return remote(a_ref.at[h], oall.at[p, h], n_send.at[h], o_recv.at[p, h], to_in)

    def s_out(i):
        q, dev = peer(i)
        return remote(s_ref.at[q], rall.at[z, p], s_send.at[i], s_recv.at[p], dev)

    for i in range(1, npl):
        begin(common, s_out, i)

    begin(common, z_copy, direct, 0, src=lambda: b_part(direct))

    @pl.when(inner)
    def _():
        begin(middle, z_copy, direct, 0, True, src=lambda: b_part(direct))

    @pl.when(outer)
    def _():
        for h in range(2):
            begin(ends, o_in, h)

    q_x = (1 - x) * nd + dep
    q_y = x * nd + (1 - y) * 2 + core
    q_d = (1 - x) * nd + (1 - y) * 2 + core

    def plane(buf, send, recv, kept):
        def copy(q, h, way, src=None):
            n = {"p": 0, "x": 1, "y": 2}[way]
            dev = {"p": partner, "x": xn, "y": yn}[way]
            dst = buf.at[q, h]
            return remote(dst if src is None else src(), dst, send.at[n, q, h], recv.at[q, h], dev)

        def first(src):
            for h in range(2):
                for way in ("x", "y", "p"):
                    begin(kept, copy, p, h, way, functools.partial(src, h))

        def second():
            copy(q_x, 0, "x").wait_recv()
            begin(kept, copy, q_x, 0, "y")
            begin(kept, copy, q_x, 0, "p")
            copy(q_y, 0, "y").wait_recv()
            begin(kept, copy, q_y, 0, "p")
            copy(q_y, 1, "y").wait_recv()
            begin(kept, copy, q_y, 1, "x")
            begin(kept, copy, q_y, 1, "p")
            copy(q_x, 1, "x").wait_recv()
            begin(kept, copy, q_x, 1, "p")

        def third():
            copy(q_d, 0, "y").wait_recv()
            copy(q_d, 0, "p").start()
            copy(q_d, 1, "x").wait_recv()
            copy(q_d, 1, "p").start()

        def last():
            for q in (p, q_x, q_y, q_d):
                other = q + 1 - 2 * core
                for h in range(2):
                    copy(other, h, "p").wait_recv()

        for h in range(2):
            kept.append(functools.partial(copy, q_d, h, "p"))
        return first, second, third, last

    a_first, a_second, a_third, a_last = plane(aall, a_send, a_recv, common)
    o_first, o_second, o_third, o_last = plane(oall, o_send, o_recv, middle)

    a_first(lambda h: a_ref.at[h])

    own_s.wait()
    for i in range(1, npl):
        q, dev = peer(i)
        remote(s_ref.at[p], rall.at[z, q], s_send.at[i], s_recv.at[q], dev).wait_recv()
    regrouped = (nc, nc + 1)
    for item in regrouped:
        begin(common, z_copy, item, 0)

    def forward(item, k, outwards):
        arrived(item, k)
        begin(middle, z_copy, item, k, outwards)

    @pl.when(inner)
    def _():
        for item in regrouped:
            begin(middle, z_copy, item, 0, True)
        forward(direct, -1, False)
        forward(direct, 1, True)

    def own_chunk(c):
        return z_copy(c, 0, src=lambda: b_part(c))

    for c in range(direct):
        begin(common, own_chunk, c)

    acc[...] = jnp.zeros_like(acc)
    pacc[...] = jnp.zeros_like(pacc)
    kb_rows = aall.shape[3]

    def chunk(s, c, kb):
        return ball[s, c, kb * kb_rows:(kb + 1) * kb_rows, :]

    def ladder_pair(k, c):
        s = z + k * inward
        for kb in range(per):
            both = jnp.concatenate([chunk(s, c, kb), chunk(s, c + 1, kb)], axis=1)

            def body(h, carry):
                r = jnp.dot(aall[s * per + kb, h], both, preferred_element_type=jnp.float32)
                acc[h, c] += r[:, :wide]
                acc[h, c + 1] += r[:, wide:]
                return carry

            lax.fori_loop(0, 2, body, 0)

    def single(total, buf, k, c):
        s = z + k * inward
        for kb in range(per):
            one = chunk(s, c, kb)

            def body(h, carry):
                total[h, c] += jnp.dot(buf[s * per + kb, h], one, preferred_element_type=jnp.float32)
                return carry

            lax.fori_loop(0, 2, body, 0)

    def p_copy(c):
        return remote(pacc.at[:, c], pin.at[:, c], p_send.at[c], p_recv.at[c], to_out)

    def cycle_all():
        cols = cyc_ref.shape[1]
        width = 1024
        rows = rall.shape[0] * rall.shape[1] * rall.shape[2]
        for lo in range(0, cols, width):
            hi = min(lo + width, cols)
            r = rall[:, :, :, lo:hi].reshape(rows, hi - lo)
            total = jnp.dot(ci_ref[...], r, preferred_element_type=jnp.float32)
            keep = rl_ref[...] == cl_ref[:, lo:hi]
            cyc_ref[:, lo:hi] = jnp.where(keep, total, 0.0).astype(cyc_ref.dtype)

    own_a.wait()
    for c in own_b:
        c.wait()
    hr = lad_ref.shape[0] // 2

    def put(h, c, value):
        lad_ref[h * hr:(h + 1) * hr, c * wide:(c + 1) * wide] = value.astype(lad_ref.dtype)

    @pl.when(inner)
    def _():
        for item in regrouped:
            forward(item, 1, True)
        for h in range(2):
            o_in(h).wait_recv()
        o_first(lambda h: oall.at[p, h])
        forward(direct, 2, True)
        for item in regrouped:
            forward(item, -1, False)
        o_second()

    a_second()

    @pl.when(inner)
    def _():
        for c in range(direct):
            forward(c, -1, False)
        for item in regrouped:
            forward(item, 2, True)

    @pl.when(outer)
    def _():
        a_third()
        a_last()
        for c in range(0, nc, 2):
            ladder_pair(0, c)
        for k in range(1, nz):
            arrived(direct, k)
            single(acc, aall, k, direct)
            for item in regrouped:
                arrived(item, k)

    cycle_all()

    @pl.when(inner)
    def _():
        o_third()
        o_last()
        for c in range(direct):
            single(pacc, oall, 0, c)
            arrived(c, 1)
            single(pacc, oall, 1, c)
            arrived(c, 2)
            single(pacc, oall, 2, c)
            begin(middle, p_copy, c)
            if c == direct - 2:
                a_third()
        a_last()
        for k in (0, -1, 1, 2):
            for c in range(0, nc, 2):
                ladder_pair(k, c)
        for h in range(2):
            for c in range(nc):
                put(h, c, acc[h, c])

    @pl.when(outer)
    def _():
        for h in range(2):
            put(h, direct, acc[h, direct])
        for c in range(direct):
            p_copy(c).wait_recv()
            for h in range(2):
                put(h, c, acc[h, c] + pin[h, c])

    for c in common:
        c().wait_send()

    @pl.when(inner)
    def _():
        for c in middle:
            c().wait_send()

    @pl.when(outer)
    def _():
        for c in ends:
            c().wait_send()


def shards(nz, npl, amplitudes, integrals, cycle_integrals, occ_irrep, vir_irrep):
    rows, kb = amplitudes.shape
    occ = rows // NO
    n = integrals.shape[1]
    occ_here = JW // npl
    columns = occ_here * NV
    crow = cycle_integrals.shape[0]
    a = amplitudes.reshape(2, rows // 2, kb)
    nc = n // 128
    b = integrals
    s = (
        amplitudes.reshape(occ, NO, kb)[:, :JW]
        .reshape(occ, npl, occ_here, kb)
        .transpose(1, 0, 2, 3)
        .reshape(npl, occ, columns)
    )
    ci = cycle_integrals.reshape(crow, nz, occ, CW).transpose(0, 1, 3, 2).reshape(crow, -1)
    row_label, col_label = masks(crow, columns, occ_irrep, vir_irrep)
    bf = jnp.bfloat16
    dma = pltpu.SemaphoreType.DMA
    return pl.pallas_call(
        kernel,
        out_shape=(
            jax.ShapeDtypeStruct((rows, n), bf),
            jax.ShapeDtypeStruct((crow, columns), bf),
        ),
        in_specs=[pl.BlockSpec(memory_space=pltpu.VMEM), pl.BlockSpec(memory_space=pl.ANY)]
        + [pl.BlockSpec(memory_space=pltpu.VMEM)] * 4,
        out_specs=(pl.BlockSpec(memory_space=pltpu.VMEM),) * 2,
        scratch_shapes=[
            pltpu.VMEM((npl, 2, rows // 2, kb), bf),
            pltpu.VMEM((npl, 2, rows // 2, kb), bf),
            pltpu.VMEM((nz, nc, integrals.shape[0], n // nc), bf),
            pltpu.VMEM((nz, npl, occ, columns), bf),
            pltpu.VMEM((2, nc, rows // 2, n // nc), jnp.float32),
            pltpu.VMEM((2, nc - 1, rows // 2, n // nc), jnp.float32),
            pltpu.VMEM((2, nc - 1, rows // 2, n // nc), jnp.float32),
            dma((2 + nc,)),
            dma((npl,)),
            dma((npl,)),
            dma((3, npl, 2)),
            dma((npl, 2)),
            dma((3, npl, 2)),
            dma((npl, 2)),
            dma((nc + 2, nz, 2)),
            dma((nc + 2, nz)),
            dma((2,)),
            dma((nc - 1,)),
            dma((nc - 1,)),
        ],
        compiler_params=pltpu.CompilerParams(
            collective_id=0, has_side_effects=True, vmem_limit_bytes=62 * 1024 * 1024
        ),
    )(a, b, s, ci, row_label, col_label)


def solution(mesh):
    nz, nx, nd = mesh.shape["row"], mesh.shape["col"], mesh.shape["depth"]
    npl = nx * nd
    if nx == 2 and nd == 4 and npl == CW and nz == 4:
        body = functools.partial(shards, nz, npl)
    else:
        body = general
    in_specs = (P("row", ("col", "depth")), P("row", ("col", "depth")), P("row", None), P(), P())
    out_specs = (P("row", ("col", "depth")), P("row", ("col", "depth")))
    return jax.shard_map(body, mesh=mesh, in_specs=in_specs, out_specs=out_specs, check_vma=False)
```

```python
import functools

import jax
import jax.numpy as jnp
from jax import lax
from jax.experimental import pallas as pl
from jax.experimental.pallas import tpu as pltpu
from jax.sharding import PartitionSpec as P

NO = 100
NV = 900
JW = 64
CW = 8
MESH = pl.DeviceIdType.MESH


def masks(rows_here, columns, occ_irrep, vir_irrep):
    occ_rows = rows_here // CW
    occ_cols = columns // NV
    occ_i = lax.dynamic_slice(occ_irrep, (lax.axis_index("row") * occ_rows,), (occ_rows,))
    occ_j = lax.dynamic_slice(occ_irrep, (lax.axis_index(("col", "depth")) * occ_cols,), (occ_cols,))
    row_label = (occ_i[:, None] ^ vir_irrep[None, :CW]).reshape(rows_here, 1)
    col_label = (occ_j[:, None] ^ vir_irrep[None, :]).reshape(1, columns)
    return row_label, col_label


def general(amplitudes, integrals, cycle_integrals, occ_irrep, vir_irrep):
    rows_here = amplitudes.shape[0]
    occ_block = rows_here // NO
    local_cols = amplitudes.shape[1]
    regroup_in = amplitudes.reshape(occ_block, NO, local_cols)[:, :JW, :]
    spread = lax.all_to_all(regroup_in, ("col", "depth"), split_axis=1, concat_axis=2, tiled=True)
    occ_here = spread.shape[1]
    columns = occ_here * NV
    ordered = (
        spread.reshape(occ_block, occ_here, CW, NV)
        .transpose(0, 2, 1, 3)
        .reshape(occ_block * CW, columns)
    )
    everyone = lax.all_gather(ordered, "row", axis=0, tiled=True)
    integ_all = lax.all_gather(integrals, "row", axis=0, tiled=True)
    ladder = jnp.dot(
        lax.all_gather(amplitudes, ("col", "depth"), axis=1, tiled=True),
        integ_all,
        preferred_element_type=jnp.float32,
    ).astype(jnp.bfloat16)
    cycle_sum = jnp.dot(cycle_integrals, everyone, preferred_element_type=jnp.float32)
    row_label, col_label = masks(cycle_integrals.shape[0], columns, occ_irrep, vir_irrep)
    cycle = jnp.where(row_label == col_label, cycle_sum, jnp.float32(0.0)).astype(jnp.bfloat16)
    return ladder, cycle


def kernel(a_ref, b_ref, s_ref, ci_ref, rl_ref, cl_ref, lad_ref, cyc_ref,
           aall, oall, ball, rall, acc, pacc, pin, loc_sem, s_send, s_recv,
           a_send, a_recv, o_send, o_recv, z_send, z_recv, n_send, p_send, p_recv):
    z = lax.axis_index("row")
    x = lax.axis_index("col")
    dep = lax.axis_index("depth")
    y, core = dep // 2, lax.rem(dep, 2)
    nd = 4
    npl = 8
    nz = rall.shape[0]
    per = npl // nz
    p = x * nd + dep
    partner = {"depth": y * 2 + 1 - core}
    xn = {"col": 1 - x}
    yn = {"depth": (1 - y) * 2 + core}
    inward = jnp.where(z < nz // 2, 1, -1)
    outer = (z == 0) | (z == nz - 1)
    inner = jnp.logical_not(outer)
    to_in = {"row": z + inward}
    to_out = {"row": z - inward}

    def remote(src, dst, ss, rs, dev):
        return pltpu.make_async_remote_copy(
            src_ref=src, dst_ref=dst, send_sem=ss, recv_sem=rs, device_id=dev, device_id_type=MESH
        )

    def peer(i):
        q = lax.rem(p + i, npl)
        return q, {"col": q // nd, "depth": lax.rem(q, nd)}

    barrier = pltpu.get_barrier_semaphore()
    for i in range(1, npl):
        pl.semaphore_signal(barrier, inc=1, device_id=peer(i)[1], device_id_type=MESH)
    pl.semaphore_signal(barrier, inc=1, device_id=to_in, device_id_type=MESH)

    @pl.when(inner)
    def _():
        pl.semaphore_signal(barrier, inc=1, device_id=to_out, device_id_type=MESH)

    own_a = pltpu.make_async_copy(a_ref, aall.at[p], loc_sem.at[0])
    wide = ball.shape[3]
    nc = ball.shape[1]
    direct = nc - 1

    def b_part(c):
        return b_ref.at[:, c * wide:(c + 1) * wide]

    own_b = [pltpu.make_async_copy(b_part(c), ball.at[z, c], loc_sem.at[2 + c]) for c in range(nc)]
    own_s = pltpu.make_async_copy(s_ref.at[p], rall.at[z, p], loc_sem.at[1])
    own_a.start()
    for c in own_b:
        c.start()
    own_s.start()
    pl.semaphore_wait(barrier, npl + inner.astype(jnp.int32))

    half = npl // 2
    common, middle, ends = [], [], []

    def begin(kept, make, *args, **kw):
        make(*args, **kw).start()
        kept.append(functools.partial(make, *args, **kw))

    def z_copy(item, k, outwards=False, src=None):
        s = z + k * inward
        if item < nc:
            dst = ball.at[s, item]
        else:
            dst = rall.at[s, pl.ds((item - nc) * half, half)]
        d = 1 if outwards else 0
        return remote(dst if src is None else src(), dst, z_send.at[item, s, d],
                      z_recv.at[item, s], to_out if outwards else to_in)

    def arrived(item, k):
        z_copy(item, k).wait_recv()

    def o_in(h):
        return remote(a_ref.at[h], oall.at[p, h], n_send.at[h], o_recv.at[p, h], to_in)

    def s_out(i):
        q, dev = peer(i)
        return remote(s_ref.at[q], rall.at[z, p], s_send.at[i], s_recv.at[p], dev)

    for i in range(1, npl):
        begin(common, s_out, i)

    begin(common, z_copy, direct, 0, src=lambda: b_part(direct))

    @pl.when(inner)
    def _():
        begin(middle, z_copy, direct, 0, True, src=lambda: b_part(direct))

    @pl.when(outer)
    def _():
        for h in range(2):
            begin(ends, o_in, h)

    q_x = (1 - x) * nd + dep
    q_y = x * nd + (1 - y) * 2 + core
    q_d = (1 - x) * nd + (1 - y) * 2 + core

    def plane(buf, send, recv, kept):
        def copy(q, h, way, src=None):
            n = {"p": 0, "x": 1, "y": 2}[way]
            dev = {"p": partner, "x": xn, "y": yn}[way]
            dst = buf.at[q, h]
            return remote(dst if src is None else src(), dst, send.at[n, q, h], recv.at[q, h], dev)

        def first(src):
            for h in range(2):
                for way in ("x", "y", "p"):
                    begin(kept, copy, p, h, way, functools.partial(src, h))

        def relay():
            for h in range(2):
                for q, way in ((q_x, "x"), (q_y, "y")):
                    copy(q, h, way).wait_recv()
                    copy(q, h, "p").start()

        def second():
            copy(q_x, 0, "y").start()
            copy(q_y, 1, "x").start()

        def third():
            copy(q_d, 0, "y").wait_recv()
            copy(q_d, 0, "p").start()
            copy(q_d, 1, "x").wait_recv()
            copy(q_d, 1, "p").start()

        def last(group):
            for q in group:
                other = q + 1 - 2 * core
                for h in range(2):
                    copy(other, h, "p").wait_recv()

        for h in range(2):
            for q in (q_x, q_y, q_d):
                kept.append(functools.partial(copy, q, h, "p"))
        kept.append(functools.partial(copy, q_x, 0, "y"))
        kept.append(functools.partial(copy, q_y, 1, "x"))
        return first, relay, second, third, last

    near = (p, q_x, q_y)

    a_first, a_relay, a_second, a_third, a_last = plane(aall, a_send, a_recv, common)
    o_first, o_relay, o_second, o_third, o_last = plane(oall, o_send, o_recv, middle)

    a_first(lambda h: a_ref.at[h])

    own_s.wait()
    for i in range(1, npl):
        q, dev = peer(i)
        remote(s_ref.at[p], rall.at[z, q], s_send.at[i], s_recv.at[q], dev).wait_recv()
    regrouped = (nc, nc + 1)
    for item in regrouped:
        begin(common, z_copy, item, 0)

    def forward(item, k, outwards):
        arrived(item, k)
        begin(middle, z_copy, item, k, outwards)

    @pl.when(inner)
    def _():
        for item in regrouped:
            begin(middle, z_copy, item, 0, True)
        forward(direct, -1, False)
        forward(direct, 1, True)

    def own_chunk(c):
        return z_copy(c, 0, src=lambda: b_part(c))

    for c in range(direct):
        begin(common, own_chunk, c)

    acc[...] = jnp.zeros_like(acc)
    pacc[...] = jnp.zeros_like(pacc)
    kb_rows = aall.shape[3]

    def chunk(s, c, kb):
        return ball[s, c, kb * kb_rows:(kb + 1) * kb_rows, :]

    def ladder_pair(k, c):
        s = z + k * inward
        for kb in range(per):
            both = jnp.concatenate([chunk(s, c, kb), chunk(s, c + 1, kb)], axis=1)

            def body(h, carry):
                r = jnp.dot(aall[s * per + kb, h], both, preferred_element_type=jnp.float32)
                acc[h, c] += r[:, :wide]
                acc[h, c + 1] += r[:, wide:]
                return carry

            lax.fori_loop(0, 2, body, 0)

    def single(total, buf, k, c):
        s = z + k * inward
        for kb in range(per):
            one = chunk(s, c, kb)

            def body(h, carry):
                total[h, c] += jnp.dot(buf[s * per + kb, h], one, preferred_element_type=jnp.float32)
                return carry

            lax.fori_loop(0, 2, body, 0)

    def p_copy(c):
        return remote(pacc.at[:, c], pin.at[:, c], p_send.at[c], p_recv.at[c], to_out)

    def cycle_all():
        cols = cyc_ref.shape[1]
        width = 1024
        rows = rall.shape[0] * rall.shape[1] * rall.shape[2]
        for lo in range(0, cols, width):
            hi = min(lo + width, cols)
            r = rall[:, :, :, lo:hi].reshape(rows, hi - lo)
            total = jnp.dot(ci_ref[...], r, preferred_element_type=jnp.float32)
            keep = rl_ref[...] == cl_ref[:, lo:hi]
            cyc_ref[:, lo:hi] = jnp.where(keep, total, 0.0).astype(cyc_ref.dtype)

    own_a.wait()
    for c in own_b:
        c.wait()
    hr = lad_ref.shape[0] // 2

    def put(h, c, value):
        lad_ref[h * hr:(h + 1) * hr, c * wide:(c + 1) * wide] = value.astype(lad_ref.dtype)

    far = (1 - x) * 2 + (1 - y)

    def slab(k, early):
        s = z + k * inward

        @pl.when((s != far) if early else (s == far))
        def _():
            for c in range(0, nc, 2):
                ladder_pair(k, c)

    @pl.when(inner)
    def _():
        for item in regrouped:
            forward(item, 1, True)
        for h in range(2):
            o_in(h).wait_recv()
        o_first(lambda h: oall.at[p, h])

    a_relay()

    @pl.when(inner)
    def _():
        forward(direct, 2, True)
        for item in regrouped:
            forward(item, -1, False)
        a_last(near)
        for c in range(direct):
            arrived(c, 1)
        slab(0, True)
        slab(1, True)
        o_relay()
        o_second()

    a_second()

    @pl.when(inner)
    def _():
        for c in range(direct):
            forward(c, -1, False)
        for item in regrouped:
            forward(item, 2, True)

    @pl.when(outer)
    def _():
        a_third()
        a_last(near + (q_d,))
        for c in range(0, nc, 2):
            ladder_pair(0, c)
        for k in range(1, nz):
            arrived(direct, k)
            single(acc, aall, k, direct)
            for item in regrouped:
                arrived(item, k)

    cycle_all()

    @pl.when(inner)
    def _():
        o_third()
        slab(-1, True)
        o_last(near + (q_d,))
        for c in range(direct):
            for k in range(2):
                single(pacc, oall, k, c)
            arrived(c, 2)
            single(pacc, oall, 2, c)
            begin(middle, p_copy, c)
            if c == direct - 2:
                a_third()
        slab(2, True)
        a_last((q_d,))
        for k in (0, -1, 1, 2):
            slab(k, False)
        for h in range(2):
            for c in range(nc):
                put(h, c, acc[h, c])

    @pl.when(outer)
    def _():
        for h in range(2):
            put(h, direct, acc[h, direct])
        for c in range(direct):
            p_copy(c).wait_recv()
            for h in range(2):
                put(h, c, acc[h, c] + pin[h, c])

    for c in common:
        c().wait_send()

    @pl.when(inner)
    def _():
        for c in middle:
            c().wait_send()

    @pl.when(outer)
    def _():
        for c in ends:
            c().wait_send()


def shards(nz, npl, amplitudes, integrals, cycle_integrals, occ_irrep, vir_irrep):
    rows, kb = amplitudes.shape
    occ = rows // NO
    n = integrals.shape[1]
    occ_here = JW // npl
    columns = occ_here * NV
    crow = cycle_integrals.shape[0]
    a = amplitudes.reshape(2, rows // 2, kb)
    nc = n // 128
    b = integrals
    s = (
        amplitudes.reshape(occ, NO, kb)[:, :JW]
        .reshape(occ, npl, occ_here, kb)
        .transpose(1, 0, 2, 3)
        .reshape(npl, occ, columns)
    )
    ci = cycle_integrals.reshape(crow, nz, occ, CW).transpose(0, 1, 3, 2).reshape(crow, -1)
    row_label, col_label = masks(crow, columns, occ_irrep, vir_irrep)
    bf = jnp.bfloat16
    dma = pltpu.SemaphoreType.DMA
    return pl.pallas_call(
        kernel,
        out_shape=(
            jax.ShapeDtypeStruct((rows, n), bf),
            jax.ShapeDtypeStruct((crow, columns), bf),
        ),
        in_specs=[pl.BlockSpec(memory_space=pl.ANY)] * 3
        + [pl.BlockSpec(memory_space=pltpu.VMEM)] * 3,
        out_specs=(pl.BlockSpec(memory_space=pltpu.VMEM),) * 2,
        scratch_shapes=[
            pltpu.VMEM((npl, 2, rows // 2, kb), bf),
            pltpu.VMEM((npl, 2, rows // 2, kb), bf),
            pltpu.VMEM((nz, nc, integrals.shape[0], n // nc), bf),
            pltpu.VMEM((nz, npl, occ, columns), bf),
            pltpu.VMEM((2, nc, rows // 2, n // nc), jnp.float32),
            pltpu.VMEM((2, nc - 1, rows // 2, n // nc), jnp.float32),
            pltpu.VMEM((2, nc - 1, rows // 2, n // nc), jnp.float32),
            dma((2 + nc,)),
            dma((npl,)),
            dma((npl,)),
            dma((3, npl, 2)),
            dma((npl, 2)),
            dma((3, npl, 2)),
            dma((npl, 2)),
            dma((nc + 2, nz, 2)),
            dma((nc + 2, nz)),
            dma((2,)),
            dma((nc - 1,)),
            dma((nc - 1,)),
        ],
        compiler_params=pltpu.CompilerParams(
            collective_id=0, has_side_effects=True, vmem_limit_bytes=62 * 1024 * 1024
        ),
    )(a, b, s, ci, row_label, col_label)


def solution(mesh):
    nz, nx, nd = mesh.shape["row"], mesh.shape["col"], mesh.shape["depth"]
    npl = nx * nd
    if nx == 2 and nd == 4 and npl == CW and nz == 4:
        body = functools.partial(shards, nz, npl)
    else:
        body = general
    in_specs = (P("row", ("col", "depth")), P("row", ("col", "depth")), P("row", None), P(), P())
    out_specs = (P("row", ("col", "depth")), P("row", ("col", "depth")))
    return jax.shard_map(body, mesh=mesh, in_specs=in_specs, out_specs=out_specs, check_vma=False)
```
